32 devices in a mesh: groups: 2 (over x), long: 16 (over z, y, core).
Axes of the slice: x: 2, y: 2, z: 4, core: 2. Of those that a mesh axis runs over, the one named last changes fastest.
Arguments:
- initial_state: float32 [2, 8192, 128], P(None, ('groups', 'long')), parts along dimension 1, may hold values from -6 to 6
- adjoint_state: float32 [2, 8192, 128], P(None, ('groups', 'long')), parts along dimension 1, may hold values from -6 to 6
- current_gates: float32 [8, 2, 128, 128], P('groups'), parts along dimension 0, may hold values from -0.375 to 0.375
Outputs:
- final_state: float32 [2, 8192, 128], P(None, ('groups', 'long')), parts along dimension 1
- final_adjoint: float32 [2, 8192, 128], P(None, ('groups', 'long')), parts along dimension 1
The draws below stay inside these ranges and needn't reach their ends.
There are 2 independent parts, one for each index of `groups`. The reference program is written for one: setup_inputs(seed, part) draws one part's arguments, and reference() takes and returns one part's arrays. A program takes and returns all parts, laid end to end along the dimension named above; each array names one. Nothing has to cross between parts.
All inputs are finite; a program needn't handle non-finite values.
Results may differ from the reference program's by a relative error of at most 0.00017.
Values sent between devices are 32-bit elements; how exact they have to be, the bound alone decides.
A program may use at most 64 MiB of HBM per device.

```python
import jax
import jax.numpy as jnp
from jax import lax

GATE = 128
SECTIONS = 4
NS_ITERS = 8
AMP_ROWS = 4096
N_LONG = 16


def level_of(own_key, extent, pieces, least, high):
    loudness, own = 1.0, jax.random.fold_in(own_key, 6)
    for position, blocks in pieces:
        draws = jnp.exp(jax.random.uniform(jax.random.fold_in(own, position), (blocks,), jnp.float32, least / len(pieces), high / len(pieces)))
        loudness = loudness * jnp.repeat(draws, extent[position] // blocks).reshape([-1 if axis == position else 1 for axis in range(len(extent))])
    return loudness


def bell_draw(key, shape, spread, bound, pieces=(), dtype=jnp.bfloat16):
    values = spread * jax.random.normal(key, shape, jnp.float32)
    if pieces:
        values = values * level_of(key, shape, pieces, -0.22, 0.18)
    return jnp.clip(values, -bound, bound).astype(dtype)


def setup_inputs(seed: int = 0, part: int = 0) -> dict:
    seeds = jax.random.split(jax.random.key(seed), 4)
    part_keys = jax.random.split(jax.random.fold_in(seeds[3], part), 4)
    initial_state = bell_draw(part_keys[0], (2, AMP_ROWS, GATE), 1.0, 6.0, ((1, 16),), jnp.float32)
    adjoint_state = bell_draw(part_keys[1], (2, AMP_ROWS, GATE), 1.0, 6.0, ((1, 16),), jnp.float32)
    current_gates = bell_draw(part_keys[2], (SECTIONS, 2, GATE, GATE), (2 * GATE) ** -0.5, 0.375, (), jnp.float32)
    return {"initial_state": initial_state, "adjoint_state": adjoint_state, "current_gates": current_gates}


HIGHEST = lax.Precision.HIGHEST

def einsum_high(pattern, left_side, right_side):
    return jnp.einsum(pattern, left_side, right_side, precision=HIGHEST, preferred_element_type=jnp.float32)

def matmul_high(left_side, right_side):
    return jnp.dot(left_side, right_side, precision=HIGHEST, preferred_element_type=jnp.float32)

def rows_product(left_side, right_side):
    return lax.dot_general(left_side, right_side, (((0,), (0,)), ((), ())), precision=HIGHEST, preferred_element_type=jnp.float32)

def polar_factor(summed_real, summed_imag, sweeps):
    norm_scale = lax.rsqrt(jnp.sum(summed_real * summed_real + summed_imag * summed_imag) + 1e-06)
    iterate_real = summed_real * norm_scale
    iterate_imag = summed_imag * norm_scale
    for sweep_index in range(sweeps):
        gram_real = rows_product(iterate_real, iterate_real) + rows_product(iterate_imag, iterate_imag)
        gram_imag = rows_product(iterate_real, iterate_imag) - rows_product(iterate_imag, iterate_real)
        product_real = matmul_high(iterate_real, gram_real) - matmul_high(iterate_imag, gram_imag)
        product_imag = matmul_high(iterate_real, gram_imag) + matmul_high(iterate_imag, gram_real)
        iterate_real = 1.5 * iterate_real - 0.5 * product_real
        iterate_imag = 1.5 * iterate_imag - 0.5 * product_imag
    return (iterate_real, iterate_imag)

def split_view(amplitudes, partner_bit):
    outer_count = N_LONG // 2 ** (partner_bit + 1)
    inner_count = amplitudes.shape[1] // (2 * outer_count)
    lane_half = amplitudes.shape[2] // 2
    return amplitudes.reshape(amplitudes.shape[0], outer_count, 2, inner_count, 2, lane_half)

def apply_gate(gate_real, gate_imag, viewed):
    lane_half = gate_real.shape[0] // 2
    blocks_real = gate_real.reshape(2, lane_half, 2, lane_half)
    blocks_imag = gate_imag.reshape(2, lane_half, 2, lane_half)
    pattern = 'acbd,hbmed->hamec'
    out_real = einsum_high(pattern, blocks_real, viewed[0]) - einsum_high(pattern, blocks_imag, viewed[1])
    out_imag = einsum_high(pattern, blocks_real, viewed[1]) + einsum_high(pattern, blocks_imag, viewed[0])
    return jnp.stack([out_real, out_imag])

def environment(adjoint_view, state_view):
    pattern = 'hamec,hbmed->acbd'
    summed_real = einsum_high(pattern, adjoint_view[0], state_view[0]) + einsum_high(pattern, adjoint_view[1], state_view[1])
    summed_imag = einsum_high(pattern, adjoint_view[1], state_view[0]) - einsum_high(pattern, adjoint_view[0], state_view[1])
    gate_width = summed_real.shape[0] * summed_real.shape[1]
    return (summed_real.reshape(gate_width, gate_width), summed_imag.reshape(gate_width, gate_width))

def reference(initial_state, adjoint_state, current_gates):
    bit_count = N_LONG.bit_length() - 1
    partner_bits = [bit_count - 1, bit_count // 2, 0, 1]
    state_now = initial_state
    adjoint_now = adjoint_state
    for section_index in range(SECTIONS):
        partner_bit = partner_bits[section_index % 4]
        state_view = split_view(state_now, partner_bit)
        adjoint_view = apply_gate(current_gates[section_index, 0], current_gates[section_index, 1], split_view(adjoint_now, partner_bit))
        summed_real, summed_imag = environment(adjoint_view, state_view)
        gate_real, gate_imag = polar_factor(summed_real, summed_imag, NS_ITERS)
        state_view = apply_gate(gate_real, gate_imag, state_view)
        state_now = state_view.reshape(initial_state.shape)
        adjoint_now = adjoint_view.reshape(adjoint_state.shape)
    return (state_now, adjoint_now)
```

```python
import functools

import jax
import jax.numpy as jnp
from jax import lax
from jax.experimental import pallas as pl
from jax.experimental.pallas import tpu as pltpu
from jax.sharding import PartitionSpec as P

SECTIONS = 4
NS_ITERS = 8
MESH = pl.DeviceIdType.MESH
ADJ_IN, PSI_IN, RS, AG, MID, ADJ_OUT, PSI_OUT = 0, 1, 2, 6, 10, 14, 15


def split(x):
    high = x.astype(jnp.bfloat16)
    return high, (x - high.astype(jnp.float32)).astype(jnp.bfloat16)


def dot3(left, right, contract):
    def dot(a, b):
        return lax.dot_general(
            a, b, (contract, ((), ())), preferred_element_type=jnp.float32
        )

    return dot(left[0], right[0]) + (dot(left[0], right[1]) + dot(left[1], right[0]))


def embed_out(real, imag):
    return jnp.concatenate(
        [
            jnp.concatenate([real, -imag], axis=1),
            jnp.concatenate([imag, real], axis=1),
        ],
        axis=0,
    )


def swap_plane(plane, q, per):
    rows, lanes = plane.shape
    stride = per << q
    rolled = pltpu.roll(plane, lanes // 2, 1)
    low = lax.broadcasted_iota(jnp.int32, (stride, lanes), 1) < lanes // 2
    blocks = []
    for start in range(0, rows, 2 * stride):
        mid, end = start + stride, start + 2 * stride
        blocks.append(jnp.where(low, plane[start:mid], rolled[mid:end]))
        blocks.append(jnp.where(low, rolled[start:mid], plane[mid:end]))
    return jnp.concatenate(blocks, axis=0)


def swap(x, q, per):
    lanes = x.shape[1] // 2
    return jnp.concatenate(
        [swap_plane(x[:, :lanes], q, per), swap_plane(x[:, lanes:], q, per)], axis=1
    )


def polar(x, sweeps):
    gate = x.shape[0]
    norm = lax.rsqrt(jnp.sum(x * x, keepdims=True) + 1e-06)

    def sweep(_, a):
        high, low = split(a)

        def embed(v):
            real, imag = v[:, :gate], v[:, gate:]
            return jnp.concatenate([v, jnp.concatenate([-imag, real], axis=1)], axis=0)

        full = (embed(high), embed(low))
        gram = dot3((high, low), full, ((1,), (1,)))
        return 1.5 * a - 0.5 * dot3(split(gram), full, ((1,), (0,)))

    return lax.fori_loop(0, sweeps, sweep, x * norm)


def kernel(
    used, order, extra_bits,
    psi_in, adj_in, gates_in, psi_out, adj_out,
    psi_buf, adj_buf, gates, phi_t, psi_send, adj_send,
    part, rs_buf, ag_buf, mid_buf,
    send_sem, recv_sem, local_sem,
):
    group = lax.axis_index("groups")
    me = lax.axis_index("long")
    n = 2 ** len(used)
    extra = 2 ** len(extra_bits)
    rows = psi_in.shape[1]
    gate = psi_in.shape[2]
    per = rows // n
    own = gate // n

    def gather(value, bits):
        out = 0
        for k, bit in enumerate(bits):
            out = out + lax.rem(lax.div(value, 2**bit), 2) * 2**k
        return out

    def scatter(value, bits):
        out = 0
        for k, bit in enumerate(bits):
            out = out + lax.rem(lax.div(value, 2**k), 2) * 2**bit
        return out

    slot = gather(me, used)
    layer = gather(me, extra_bits)

    def peer(j):
        return scatter(j, used) + scatter(layer, extra_bits)

    def layer_peer(j):
        return scatter(slot, used) + scatter(j, extra_bits)

    def others(fn, mine=slot, count=n):
        def step(off, carry):
            fn(lax.rem(mine + off, count))
            return carry

        lax.fori_loop(1, count, step, 0)

    def remote(src, dst, phase, there, here, target):
        return pltpu.make_async_remote_copy(
            src_ref=src,
            dst_ref=dst,
            send_sem=send_sem.at[phase, there],
            recv_sem=recv_sem.at[phase, here],
            device_id={"groups": group, "long": target},
            device_id_type=MESH,
        )

    def block(ref, j, size):
        return ref.at[:, pl.ds(pl.multiple_of(j * size, size), size), :]

    def send_all(src, dst, phase, size):
        others(lambda j: remote(block(src, j, size), block(dst, slot, size), phase, j, slot, peer(j)).start())

    def recv_all(dst, phase, size):
        others(lambda j: remote(block(dst, j, size), block(dst, j, size), phase, j, j, peer(j)).wait_recv())

    def sent_all(src, phase, size):
        others(lambda j: remote(block(src, j, size), block(src, j, size), phase, j, j, peer(j)).wait_send())

    gate_copy = pltpu.make_async_copy(gates_in, gates, local_sem.at[0])
    adj_own = pltpu.make_async_copy(block(adj_in, slot, per), block(adj_buf, slot, per), local_sem.at[1])
    psi_own = pltpu.make_async_copy(block(psi_in, slot, per), block(psi_buf, slot, per), local_sem.at[2])
    adj_own.start()
    gate_copy.start()
    psi_own.start()

    barrier = pltpu.get_barrier_semaphore()
    others(lambda j: pl.semaphore_signal(barrier, inc=1, device_id={"groups": group, "long": peer(j)}, device_id_type=MESH))
    if extra > 1:
        others(
            lambda j: pl.semaphore_signal(barrier, inc=1, device_id={"groups": group, "long": layer_peer(j)}, device_id_type=MESH),
            layer, extra,
        )
    pl.semaphore_wait(barrier, n + extra - 2)

    send_all(adj_in, adj_buf, ADJ_IN, per)
    send_all(psi_in, psi_buf, PSI_IN, per)

    def joined(ref):
        return jnp.concatenate([ref[0], ref[1]], axis=1)

    def advance_adjoint(phi, s):
        full = split(embed_out(gates[s, 0], gates[s, 1]))
        phi = dot3(split(phi), full, ((1,), (1,)))
        high, low = split(phi.T)
        phi_t[0] = high
        phi_t[1] = low
        return phi

    gate_copy.wait()
    adj_own.wait()
    recv_all(adj_buf, ADJ_IN, per)
    phi = advance_adjoint(swap(joined(adj_buf), order[0], per), 0)
    psi_own.wait()
    recv_all(psi_buf, PSI_IN, per)
    psi = swap(joined(psi_buf), order[0], per)

    for s in range(SECTIONS):
        state = split(psi)
        outer = dot3((phi_t[0], phi_t[1]), state, ((1,), (0,)))
        part[s, 0] = outer[:gate, :gate] + outer[gate:, gate:]
        part[s, 1] = outer[gate:, :gate] - outer[:gate, gate:]
        others(
            lambda j: remote(block(part.at[s], j, own), rs_buf.at[s, slot], RS + s, j, slot, peer(j)).start()
        )
        if s + 1 < SECTIONS:
            phi = advance_adjoint(swap(phi, order[s + 1], per), s + 1)
        others(
            lambda j: remote(rs_buf.at[s, j], rs_buf.at[s, j], RS + s, j, j, peer(j)).wait_recv()
        )
        mine = pl.ds(pl.multiple_of(slot * own, own), own)
        rs_buf[s, slot] = part[s, :, mine, :]
        total = rs_buf[s, 0]
        for j in range(1, n):
            total = total + rs_buf[s, j]
        if extra > 1:
            mid_buf[s, layer] = total
            others(
                lambda j: remote(mid_buf.at[s, layer], mid_buf.at[s, layer], MID + s, j, layer, layer_peer(j)).start(),
                layer, extra,
            )
            others(
                lambda j: remote(mid_buf.at[s, j], mid_buf.at[s, j], MID + s, j, j, layer_peer(j)).wait_recv(),
                layer, extra,
            )
            total = mid_buf[s, 0]
            for j in range(1, extra):
                total = total + mid_buf[s, j]
        ag_buf[s, :, mine, :] = total
        held = block(ag_buf.at[s], slot, own)
        others(lambda j: remote(held, held, AG + s, j, slot, peer(j)).start())
        if s + 2 == SECTIONS:
            back = phi
            for q in order[::-1]:
                back = swap(back, q, per)
            adj_send[0] = back[:, :gate]
            adj_send[1] = back[:, gate:]
        recv_all(ag_buf.at[s], AG + s, own)
        if s + 2 == SECTIONS:
            send_all(adj_send, adj_out, ADJ_OUT, per)
        fitted = polar(jnp.concatenate([ag_buf[s, 0], ag_buf[s, 1]], axis=1), NS_ITERS)
        full = split(embed_out(fitted[:, :gate], fitted[:, gate:]))
        psi = dot3(state, full, ((1,), (1,)))
        if s + 1 < SECTIONS:
            psi = swap(psi, order[s + 1], per)

    for q in order[::-1]:
        psi = swap(psi, q, per)
    psi_send[0] = psi[:, :gate]
    psi_send[1] = psi[:, gate:]
    send_all(psi_send, psi_out, PSI_OUT, per)
    psi_back = pltpu.make_async_copy(block(psi_send, slot, per), block(psi_out, slot, per), local_sem.at[2])
    adj_back = pltpu.make_async_copy(block(adj_send, slot, per), block(adj_out, slot, per), local_sem.at[1])
    psi_back.start()
    adj_back.start()
    sent_all(adj_in, ADJ_IN, per)
    sent_all(psi_in, PSI_IN, per)
    for s in range(SECTIONS):
        sent_all(part.at[s], RS + s, own)
        sent_all(ag_buf.at[s], AG + s, own)
        if extra > 1:
            others(
                lambda j: remote(mid_buf.at[s, layer], mid_buf.at[s, layer], MID + s, j, j, layer_peer(j)).wait_send(),
                layer, extra,
            )
    sent_all(adj_send, ADJ_OUT, per)
    recv_all(adj_out, ADJ_OUT, per)
    adj_back.wait()
    psi_back.wait()
    sent_all(psi_send, PSI_OUT, per)
    recv_all(psi_out, PSI_OUT, per)


def shards(initial_state, adjoint_state, current_gates):
    bit_count = lax.axis_size("long").bit_length() - 1
    partner_bits = [bit_count - 1, bit_count // 2, 0, 1]
    used = sorted(set(partner_bits))
    assert len(used) == SECTIONS
    order = [used.index(bit) for bit in partner_bits]
    extra_bits = [bit for bit in range(bit_count) if bit not in used]
    n, extra = 2 ** len(used), 2 ** len(extra_bits)
    planes, rows, gate = initial_state.shape
    own = gate // n
    f32, bf16 = jnp.float32, jnp.bfloat16
    anywhere = pl.BlockSpec(memory_space=pl.ANY)
    return tuple(
        pl.pallas_call(
            functools.partial(kernel, used, order, extra_bits),
            out_shape=[jax.ShapeDtypeStruct(initial_state.shape, f32)] * 2,
            in_specs=[anywhere] * 3,
            out_specs=[anywhere] * 2,
            scratch_shapes=[
                pltpu.VMEM((2, rows, gate), f32),
                pltpu.VMEM((2, rows, gate), f32),
                pltpu.VMEM(current_gates.shape, f32),
                pltpu.VMEM((2, 2 * gate, rows), bf16),
                pltpu.VMEM((2, rows, gate), f32),
                pltpu.VMEM((2, rows, gate), f32),
                pltpu.VMEM((SECTIONS, 2, gate, gate), f32),
                pltpu.VMEM((SECTIONS, n, 2, own, gate), f32),
                pltpu.VMEM((SECTIONS, 2, gate, gate), f32),
                pltpu.VMEM((SECTIONS, extra, 2, own, gate), f32),
                pltpu.SemaphoreType.DMA((16, max(n, extra))),
                pltpu.SemaphoreType.DMA((16, max(n, extra))),
                pltpu.SemaphoreType.DMA((3,)),
            ],
            compiler_params=pltpu.CompilerParams(collective_id=0, has_side_effects=True),
            name="sweep",
        )(initial_state, adjoint_state, current_gates)
    )


def solution(mesh):
    return jax.shard_map(
        shards,
        mesh=mesh,
        in_specs=(
            P(None, ("groups", "long"), None),
            P(None, ("groups", "long"), None),
            P("groups", None, None, None),
        ),
        out_specs=(P(None, ("groups", "long"), None), P(None, ("groups", "long"), None)),
        check_vma=False,
    )
```

```python
import functools

import jax
import jax.numpy as jnp
from jax import lax
from jax.experimental import pallas as pl
from jax.experimental.pallas import tpu as pltpu
from jax.sharding import PartitionSpec as P

SECTIONS = 4
NS_ITERS = 8
MESH = pl.DeviceIdType.MESH
ADJ_IN, PSI_IN, RS, AG, MID, ADJ_OUT, PSI_OUT = 0, 1, 2, 6, 10, 14, 15


def split(x):
    high = x.astype(jnp.bfloat16)
    return high, (x - high.astype(jnp.float32)).astype(jnp.bfloat16)


def dot3(left, right, contract):
    def dot(a, b):
        return lax.dot_general(
            a, b, (contract, ((), ())), preferred_element_type=jnp.float32
        )

    return dot(left[0], right[0]) + (dot(left[0], right[1]) + dot(left[1], right[0]))


def embed_out(real, imag):
    return jnp.concatenate(
        [
            jnp.concatenate([real, -imag], axis=1),
            jnp.concatenate([imag, real], axis=1),
        ],
        axis=0,
    )


def swap_plane(plane, q, per):
    rows, lanes = plane.shape
    stride = per << q
    rolled = pltpu.roll(plane, lanes // 2, 1)
    low = lax.broadcasted_iota(jnp.int32, (stride, lanes), 1) < lanes // 2
    blocks = []
    for start in range(0, rows, 2 * stride):
        mid, end = start + stride, start + 2 * stride
        blocks.append(jnp.where(low, plane[start:mid], rolled[mid:end]))
        blocks.append(jnp.where(low, rolled[start:mid], plane[mid:end]))
    return jnp.concatenate(blocks, axis=0)


def swap(x, q, per):
    lanes = x.shape[1] // 2
    return jnp.concatenate(
        [swap_plane(x[:, :lanes], q, per), swap_plane(x[:, lanes:], q, per)], axis=1
    )


def polar(x, sweeps):
    gate = x.shape[0]
    norm = lax.rsqrt(jnp.sum(x * x, keepdims=True) + 1e-06)

    def sweep(_, a):
        high, low = split(a)

        def embed(v):
            real, imag = v[:, :gate], v[:, gate:]
            return jnp.concatenate([v, jnp.concatenate([-imag, real], axis=1)], axis=0)

        full = (embed(high), embed(low))
        gram = dot3((high, low), full, ((1,), (1,)))
        return 1.5 * a - 0.5 * dot3(split(gram), full, ((1,), (0,)))

    return lax.fori_loop(0, sweeps, sweep, x * norm)


def kernel(
    used, order, extra_bits,
    psi_in, adj_in, gates_in, psi_out, adj_out,
    psi_buf, adj_buf, gates, phi_t, psi_send, adj_send,
    part, rs_buf, ag_buf, mid_buf,
    send_sem, recv_sem, local_sem,
):
    group = lax.axis_index("groups")
    me = lax.axis_index("long")
    n = 2 ** len(used)
    extra = 2 ** len(extra_bits)
    rows = psi_in.shape[1]
    gate = psi_in.shape[2]
    per = rows // n
    owners = n // 2
    first = n // 4
    own = gate // owners

    def gather(value, bits):
        out = 0
        for k, bit in enumerate(bits):
            out = out + lax.rem(lax.div(value, 2**bit), 2) * 2**k
        return out

    def scatter(value, bits):
        out = 0
        for k, bit in enumerate(bits):
            out = out + lax.rem(lax.div(value, 2**k), 2) * 2**bit
        return out

    slot = gather(me, used)
    layer = gather(me, extra_bits)

    def peer(j):
        return scatter(j, used) + scatter(layer, extra_bits)

    def layer_peer(j):
        return scatter(slot, used) + scatter(j, extra_bits)

    def others(fn, mine=slot, count=n):
        def step(off, carry):
            fn(lax.rem(mine + off, count))
            return carry

        lax.fori_loop(1, count, step, 0)

    quarter = n // 4
    column = lax.div(slot, quarter)
    upper = lax.div(column, 2)
    inner = column + upper * (3 - 2 * column)

    def far_first(fn):
        for rank, place in enumerate((3, 2, 1 - inner, inner)):
            base = (place + upper * (3 - 2 * place)) * quarter

            def step(k, carry):
                fn(base + lax.rem(slot + 1 + k, quarter))
                return carry

            lax.fori_loop(0, quarter - (rank == 3), step, 0)

    def owners_far_first(fn):
        for rank in range(2):
            base = (2 - rank + upper * (2 * rank - 1)) * quarter

            def step(k, carry):
                fn(base + lax.rem(slot + 1 + k, quarter))
                return carry

            lax.fori_loop(0, quarter - rank, step, 0)

            if rank == 1:

                @pl.when(jnp.logical_not(is_owner))
                def _():
                    fn(base + lax.rem(slot, quarter))

    is_owner = inner == 1

    def remote(src, dst, phase, there, here, target):
        return pltpu.make_async_remote_copy(
            src_ref=src,
            dst_ref=dst,
            send_sem=send_sem.at[phase, there],
            recv_sem=recv_sem.at[phase, here],
            device_id={"groups": group, "long": target},
            device_id_type=MESH,
        )

    def block(ref, j, size):
        return ref.at[:, pl.ds(pl.multiple_of(j * size, size), size), :]

    def send_all(src, dst, phase, size):
        far_first(lambda j: remote(block(src, j, size), block(dst, slot, size), phase, j, slot, peer(j)).start())

    def recv_all(dst, phase, size):
        others(lambda j: remote(block(dst, j, size), block(dst, j, size), phase, j, j, peer(j)).wait_recv())

    def sent_all(src, phase, size):
        others(lambda j: remote(block(src, j, size), block(src, j, size), phase, j, j, peer(j)).wait_send())

    gate_copy = pltpu.make_async_copy(gates_in, gates, local_sem.at[0])
    adj_own = pltpu.make_async_copy(block(adj_in, slot, per), block(adj_buf, slot, per), local_sem.at[1])
    psi_own = pltpu.make_async_copy(block(psi_in, slot, per), block(psi_buf, slot, per), local_sem.at[2])
    adj_own.start()
    gate_copy.start()
    psi_own.start()

    barrier = pltpu.get_barrier_semaphore()
    others(lambda j: pl.semaphore_signal(barrier, inc=1, device_id={"groups": group, "long": peer(j)}, device_id_type=MESH))
    if extra > 1:
        others(
            lambda j: pl.semaphore_signal(barrier, inc=1, device_id={"groups": group, "long": layer_peer(j)}, device_id_type=MESH),
            layer, extra,
        )
    pl.semaphore_wait(barrier, n + extra - 2)

    send_all(adj_in, adj_buf, ADJ_IN, per)
    send_all(psi_in, psi_buf, PSI_IN, per)

    def joined(ref):
        return jnp.concatenate([ref[0], ref[1]], axis=1)

    def advance_adjoint(phi, s):
        full = split(embed_out(gates[s, 0], gates[s, 1]))
        phi = dot3(split(phi), full, ((1,), (1,)))
        high, low = split(phi.T)
        phi_t[0] = high
        phi_t[1] = low
        return phi

    gate_copy.wait()
    adj_own.wait()
    recv_all(adj_buf, ADJ_IN, per)
    phi = advance_adjoint(swap(joined(adj_buf), order[0], per), 0)
    psi_own.wait()
    recv_all(psi_buf, PSI_IN, per)
    psi = swap(joined(psi_buf), order[0], per)

    for s in range(SECTIONS):
        state = split(psi)
        outer = dot3((phi_t[0], phi_t[1]), state, ((1,), (0,)))
        part[s, 0] = outer[:gate, :gate] + outer[gate:, gate:]
        part[s, 1] = outer[gate:, :gate] - outer[:gate, gate:]
        owners_far_first(
            lambda j: remote(block(part.at[s], j - first, own), rs_buf.at[s, slot], RS + s, j, slot, peer(j)).start()
        )
        if s + 1 < SECTIONS:
            phi = advance_adjoint(swap(phi, order[s + 1], per), s + 1)

        @pl.when(is_owner)
        def _():
            mine = pl.ds(pl.multiple_of((slot - first) * own, own), own)
            others(
                lambda j: remote(rs_buf.at[s, j], rs_buf.at[s, j], RS + s, j, j, peer(j)).wait_recv()
            )
            rs_buf[s, slot] = part[s, :, mine, :]
            total = rs_buf[s, 0]
            for j in range(1, n):
                total = total + rs_buf[s, j]
            if extra > 1:
                mid_buf[s, layer] = total
                others(
                    lambda j: remote(mid_buf.at[s, layer], mid_buf.at[s, layer], MID + s, j, layer, layer_peer(j)).start(),
                    layer, extra,
                )
                others(
                    lambda j: remote(mid_buf.at[s, j], mid_buf.at[s, j], MID + s, j, j, layer_peer(j)).wait_recv(),
                    layer, extra,
                )
                total = mid_buf[s, 0]
                for j in range(1, extra):
                    total = total + mid_buf[s, j]
            ag_buf[s, :, mine, :] = total
            held = block(ag_buf.at[s], slot - first, own)
            far_first(lambda j: remote(held, held, AG + s, j, slot, peer(j)).start())

        if s + 2 == SECTIONS:
            back = phi
            for q in order[::-1]:
                back = swap(back, q, per)
            adj_send[0] = back[:, :gate]
            adj_send[1] = back[:, gate:]

        def arrive(j):
            held = block(ag_buf.at[s], j - first, own)
            remote(held, held, AG + s, j, j, peer(j)).wait_recv()

        owners_far_first(arrive)
        if s + 2 == SECTIONS:
            send_all(adj_send, adj_out, ADJ_OUT, per)
        fitted = polar(jnp.concatenate([ag_buf[s, 0], ag_buf[s, 1]], axis=1), NS_ITERS)
        full = split(embed_out(fitted[:, :gate], fitted[:, gate:]))
        psi = dot3(state, full, ((1,), (1,)))
        if s + 1 < SECTIONS:
            psi = swap(psi, order[s + 1], per)

    for q in order[::-1]:
        psi = swap(psi, q, per)
    psi_send[0] = psi[:, :gate]
    psi_send[1] = psi[:, gate:]
    send_all(psi_send, psi_out, PSI_OUT, per)
    psi_back = pltpu.make_async_copy(block(psi_send, slot, per), block(psi_out, slot, per), local_sem.at[2])
    adj_back = pltpu.make_async_copy(block(adj_send, slot, per), block(adj_out, slot, per), local_sem.at[1])
    psi_back.start()
    adj_back.start()
    sent_all(adj_in, ADJ_IN, per)
    sent_all(psi_in, PSI_IN, per)
    for s in range(SECTIONS):

        def left(j):
            held = block(part.at[s], j - first, own)
            remote(held, held, RS + s, j, j, peer(j)).wait_send()

        owners_far_first(left)

        @pl.when(is_owner)
        def _():
            held = block(ag_buf.at[s], slot - first, own)
            others(lambda j: remote(held, held, AG + s, j, j, peer(j)).wait_send())
            if extra > 1:
                others(
                    lambda j: remote(mid_buf.at[s, layer], mid_buf.at[s, layer], MID + s, j, j, layer_peer(j)).wait_send(),
                    layer, extra,
                )

    sent_all(adj_send, ADJ_OUT, per)
    recv_all(adj_out, ADJ_OUT, per)
    adj_back.wait()
    psi_back.wait()
    sent_all(psi_send, PSI_OUT, per)
    recv_all(psi_out, PSI_OUT, per)


def shards(initial_state, adjoint_state, current_gates):
    bit_count = lax.axis_size("long").bit_length() - 1
    partner_bits = [bit_count - 1, bit_count // 2, 0, 1]
    used = sorted(set(partner_bits))
    assert len(used) == SECTIONS
    order = [used.index(bit) for bit in partner_bits]
    extra_bits = [bit for bit in range(bit_count) if bit not in used]
    n, extra = 2 ** len(used), 2 ** len(extra_bits)
    planes, rows, gate = initial_state.shape
    own = gate // (n // 2)
    f32, bf16 = jnp.float32, jnp.bfloat16
    anywhere = pl.BlockSpec(memory_space=pl.ANY)
    return tuple(
        pl.pallas_call(
            functools.partial(kernel, used, order, extra_bits),
            out_shape=[jax.ShapeDtypeStruct(initial_state.shape, f32)] * 2,
            in_specs=[anywhere] * 3,
            out_specs=[anywhere] * 2,
            scratch_shapes=[
                pltpu.VMEM((2, rows, gate), f32),
                pltpu.VMEM((2, rows, gate), f32),
                pltpu.VMEM(current_gates.shape, f32),
                pltpu.VMEM((2, 2 * gate, rows), bf16),
                pltpu.VMEM((2, rows, gate), f32),
                pltpu.VMEM((2, rows, gate), f32),
                pltpu.VMEM((SECTIONS, 2, gate, gate), f32),
                pltpu.VMEM((SECTIONS, n, 2, own, gate), f32),
                pltpu.VMEM((SECTIONS, 2, gate, gate), f32),
                pltpu.VMEM((SECTIONS, extra, 2, own, gate), f32),
                pltpu.SemaphoreType.DMA((16, max(n, extra))),
                pltpu.SemaphoreType.DMA((16, max(n, extra))),
                pltpu.SemaphoreType.DMA((3,)),
            ],
            compiler_params=pltpu.CompilerParams(collective_id=0, has_side_effects=True),
            name="sweep",
        )(initial_state, adjoint_state, current_gates)
    )


def solution(mesh):
    return jax.shard_map(
        shards,
        mesh=mesh,
        in_specs=(
            P(None, ("groups", "long"), None),
            P(None, ("groups", "long"), None),
            P("groups", None, None, None),
        ),
        out_specs=(P(None, ("groups", "long"), None), P(None, ("groups", "long"), None)),
        check_vma=False,
    )
```

```python
import functools

import jax
import jax.numpy as jnp
from jax import lax
from jax.experimental import pallas as pl
from jax.experimental.pallas import tpu as pltpu
from jax.sharding import PartitionSpec as P

SECTIONS = 4
NS_ITERS = 8
MESH = pl.DeviceIdType.MESH
ADJ_IN, PSI_IN, RS, AG, MID, ADJ_OUT, PSI_OUT = 0, 1, 2, 6, 10, 14, 15


def split(x):
    high = x.astype(jnp.bfloat16)
    return high, (x - high.astype(jnp.float32)).astype(jnp.bfloat16)


def dot3(left, right, contract):
    def dot(a, b):
        return lax.dot_general(
            a, b, (contract, ((), ())), preferred_element_type=jnp.float32
        )

    return dot(left[0], right[0]) + (dot(left[0], right[1]) + dot(left[1], right[0]))


def embed_out(real, imag):
    return jnp.concatenate(
        [
            jnp.concatenate([real, -imag], axis=1),
            jnp.concatenate([imag, real], axis=1),
        ],
        axis=0,
    )


def swap_plane(plane, q, per):
    rows, lanes = plane.shape
    stride = per << q
    rolled = pltpu.roll(plane, lanes // 2, 1)
    low = lax.broadcasted_iota(jnp.int32, (stride, lanes), 1) < lanes // 2
    blocks = []
    for start in range(0, rows, 2 * stride):
        mid, end = start + stride, start + 2 * stride
        blocks.append(jnp.where(low, plane[start:mid], rolled[mid:end]))
        blocks.append(jnp.where(low, rolled[start:mid], plane[mid:end]))
    return jnp.concatenate(blocks, axis=0)


def swap(x, q, per):
    lanes = x.shape[1] // 2
    return jnp.concatenate(
        [swap_plane(x[:, :lanes], q, per), swap_plane(x[:, lanes:], q, per)], axis=1
    )


def polar(x, sweeps):
    gate = x.shape[0]
    norm = lax.rsqrt(jnp.sum(x * x, keepdims=True) + 1e-06)

    def sweep(_, a):
        high, low = split(a)

        def embed(v):
            real, imag = v[:, :gate], v[:, gate:]
            return jnp.concatenate([v, jnp.concatenate([-imag, real], axis=1)], axis=0)

        full = (embed(high), embed(low))
        def product(left, axis):
            def dot(u, v):
                return lax.dot_general(
                    u, v, (((1,), (axis,)), ((), ())), preferred_element_type=jnp.float32
                )

            both = dot(jnp.concatenate(left, axis=0), full[0])
            return both[:gate] + (both[gate:] + dot(left[0], full[1]))

        gram = product((high, low), 1)
        return 1.5 * a - 0.5 * product(split(gram), 0)

    return lax.fori_loop(0, sweeps, sweep, x * norm)


def kernel(
    used, order, extra_bits,
    psi_in, adj_in, gates_in, psi_out, adj_out,
    psi_buf, adj_buf, gates, phi_t, psi_send, adj_send,
    part, rs_buf, ag_buf, mid_buf,
    send_sem, recv_sem, local_sem,
):
    group = lax.axis_index("groups")
    me = lax.axis_index("long")
    n = 2 ** len(used)
    extra = 2 ** len(extra_bits)
    rows = psi_in.shape[1]
    gate = psi_in.shape[2]
    owners = n // 2
    first = n // 4
    own = gate // owners
    per = rows // owners

    def gather(value, bits):
        out = 0
        for k, bit in enumerate(bits):
            out = out + lax.rem(lax.div(value, 2**bit), 2) * 2**k
        return out

    def scatter(value, bits):
        out = 0
        for k, bit in enumerate(bits):
            out = out + lax.rem(lax.div(value, 2**k), 2) * 2**bit
        return out

    slot = gather(me, used)
    layer = gather(me, extra_bits)

    def peer(j):
        return scatter(j, used) + scatter(layer, extra_bits)

    def layer_peer(j):
        return scatter(slot, used) + scatter(j, extra_bits)

    def others(fn, mine=slot, count=n):
        def step(off, carry):
            fn(lax.rem(mine + off, count))
            return carry

        lax.fori_loop(1, count, step, 0)

    quarter = n // 4
    column = lax.div(slot, quarter)
    upper = lax.div(column, 2)
    inner = column + upper * (3 - 2 * column)

    def far_first(fn):
        for rank, place in enumerate((3, 2, 1 - inner, inner)):
            base = (place + upper * (3 - 2 * place)) * quarter

            def step(k, carry):
                fn(base + lax.rem(slot + 1 + k, quarter))
                return carry

            lax.fori_loop(0, quarter - (rank == 3), step, 0)

    def owners_far_first(fn, among=False):
        for rank in range(2):
            base = (2 - rank + upper * (2 * rank - 1)) * quarter

            def step(k, carry):
                fn(base + lax.rem(slot + 1 + k, quarter))
                return carry

            lax.fori_loop(0, quarter - rank, step, 0)

            if rank == 1 and not among:

                @pl.when(jnp.logical_not(is_owner))
                def _():
                    fn(base + lax.rem(slot, quarter))

    is_owner = inner == 1

    def remote(src, dst, phase, there, here, target):
        return pltpu.make_async_remote_copy(
            src_ref=src,
            dst_ref=dst,
            send_sem=send_sem.at[phase, there],
            recv_sem=recv_sem.at[phase, here],
            device_id={"groups": group, "long": target},
            device_id_type=MESH,
        )

    def block(ref, j, size):
        return ref.at[:, pl.ds(pl.multiple_of(j * size, size), size), :]

    index = slot - first

    def signal(j, target):
        pl.semaphore_signal(
            barrier, inc=1, device_id={"groups": group, "long": target(j)}, device_id_type=MESH
        )

    barrier = pltpu.get_barrier_semaphore()

    @pl.when(is_owner)
    def _():
        far_first(lambda j: signal(j, peer))
        if extra > 1:
            others(lambda j: signal(j, layer_peer), layer, extra)
        pl.semaphore_wait(barrier, n + extra - 2)

    @pl.when(jnp.logical_not(is_owner))
    def _():
        owners_far_first(lambda j: signal(j, peer))
        pl.semaphore_wait(barrier, owners)

    def inward(src, dst, phase):
        return lambda j: remote(
            block(src, j - first, per), block(dst, slot, per), phase, j, slot, peer(j)
        )

    def inward_from(dst, phase):
        return lambda j: remote(block(dst, j, per), block(dst, j, per), phase, j, j, peer(j))

    def outward(src, dst, phase):
        return lambda j: remote(
            block(src, j, per), block(dst, index, per), phase, j, slot, peer(j)
        )

    def outward_from(dst, phase):
        return lambda j: remote(
            block(dst, j - first, per), block(dst, j - first, per), phase, j, j, peer(j)
        )

    owners_far_first(lambda j: inward(adj_in, adj_buf, ADJ_IN)(j).start())
    owners_far_first(lambda j: inward(psi_in, psi_buf, PSI_IN)(j).start())

    def joined(ref):
        return jnp.concatenate([ref[0], ref[1]], axis=1)

    def put(ref, x):
        for q in order[::-1]:
            x = swap(x, q, per)
        ref[0] = x[:, :gate]
        ref[1] = x[:, gate:]

    def advance_adjoint(phi, s):
        full = split(embed_out(gates[s, 0], gates[s, 1]))
        phi = dot3(split(phi), full, ((1,), (1,)))
        high, low = split(phi.T)
        phi_t[0] = high
        phi_t[1] = low
        return phi

    @pl.when(is_owner)
    def _():
        gate_copy = pltpu.make_async_copy(gates_in, gates, local_sem.at[0])
        adj_own = pltpu.make_async_copy(block(adj_in, index, per), block(adj_buf, slot, per), local_sem.at[1])
        psi_own = pltpu.make_async_copy(block(psi_in, index, per), block(psi_buf, slot, per), local_sem.at[2])
        gate_copy.start()
        adj_own.start()
        psi_own.start()
        mine = pl.ds(pl.multiple_of(index * own, own), own)

        gate_copy.wait()
        adj_own.wait()
        others(lambda j: inward_from(adj_buf, ADJ_IN)(j).wait_recv())
        phi = advance_adjoint(swap(joined(adj_buf), order[0], per), 0)
        psi_own.wait()
        others(lambda j: inward_from(psi_buf, PSI_IN)(j).wait_recv())
        psi = swap(joined(psi_buf), order[0], per)

        for s in range(SECTIONS):
            state = split(psi)
            outer = dot3((phi_t[0], phi_t[1]), state, ((1,), (0,)))
            part[s, 0] = outer[:gate, :gate] + outer[gate:, gate:]
            part[s, 1] = outer[gate:, :gate] - outer[:gate, gate:]

            def to_owner(j):
                return remote(
                    block(part.at[s], j - first, own), rs_buf.at[s, index], RS + s, j, slot, peer(j)
                )

            def from_owner(j):
                held = rs_buf.at[s, j - first]
                return remote(held, held, RS + s, j, j, peer(j))

            owners_far_first(lambda j: to_owner(j).start(), True)
            if s + 1 < SECTIONS:
                phi = advance_adjoint(swap(phi, order[s + 1], per), s + 1)
            owners_far_first(lambda j: from_owner(j).wait_recv(), True)
            rs_buf[s, index] = part[s, :, mine, :]
            total = rs_buf[s, 0]
            for j in range(1, owners):
                total = total + rs_buf[s, j]
            if extra > 1:
                mid_buf[s, layer] = total

                def across(j, here):
                    held = mid_buf.at[s, here]
                    return remote(held, held, MID + s, j, here, layer_peer(j))

                others(lambda j: across(j, layer).start(), layer, extra)
                others(lambda j: across(j, j).wait_recv(), layer, extra)
                total = mid_buf[s, 0]
                for j in range(1, extra):
                    total = total + mid_buf[s, j]
            ag_buf[s, :, mine, :] = total
            held = block(ag_buf.at[s], index, own)
            owners_far_first(lambda j: remote(held, held, AG + s, j, slot, peer(j)).start(), True)
            if s + 2 == SECTIONS:
                put(adj_send, phi)

            def arrive(j):
                there = block(ag_buf.at[s], j - first, own)
                remote(there, there, AG + s, j, j, peer(j)).wait_recv()

            owners_far_first(arrive, True)
            if s + 2 == SECTIONS:
                far_first(lambda j: outward(adj_send, adj_out, ADJ_OUT)(j).start())
                adj_back = pltpu.make_async_copy(block(adj_send, slot, per), block(adj_out, index, per), local_sem.at[1])
                adj_back.start()
            fitted = polar(jnp.concatenate([ag_buf[s, 0], ag_buf[s, 1]], axis=1), NS_ITERS)
            full = split(embed_out(fitted[:, :gate], fitted[:, gate:]))
            psi = dot3(state, full, ((1,), (1,)))
            if s + 1 < SECTIONS:
                psi = swap(psi, order[s + 1], per)

        put(psi_send, psi)
        far_first(lambda j: outward(psi_send, psi_out, PSI_OUT)(j).start())
        psi_back = pltpu.make_async_copy(block(psi_send, slot, per), block(psi_out, index, per), local_sem.at[2])
        psi_back.start()
        for s in range(SECTIONS):
            owners_far_first(
                lambda j: remote(block(part.at[s], j - first, own), rs_buf.at[s, index], RS + s, j, slot, peer(j)).wait_send(),
                True,
            )
            sent = block(ag_buf.at[s], index, own)
            owners_far_first(lambda j: remote(sent, sent, AG + s, j, slot, peer(j)).wait_send(), True)
            if extra > 1:
                done = mid_buf.at[s, layer]
                others(lambda j: remote(done, done, MID + s, j, layer, layer_peer(j)).wait_send(), layer, extra)
        adj_back.wait()
        psi_back.wait()
        others(lambda j: outward(adj_send, adj_out, ADJ_OUT)(j).wait_send())
        others(lambda j: outward(psi_send, psi_out, PSI_OUT)(j).wait_send())

    owners_far_first(lambda j: inward(adj_in, adj_buf, ADJ_IN)(j).wait_send())
    owners_far_first(lambda j: inward(psi_in, psi_buf, PSI_IN)(j).wait_send())
    owners_far_first(lambda j: outward_from(adj_out, ADJ_OUT)(j).wait_recv())
    owners_far_first(lambda j: outward_from(psi_out, PSI_OUT)(j).wait_recv())


def shards(initial_state, adjoint_state, current_gates):
    bit_count = lax.axis_size("long").bit_length() - 1
    partner_bits = [bit_count - 1, bit_count // 2, 0, 1]
    used = sorted(set(partner_bits))
    assert len(used) == SECTIONS
    order = [used.index(bit) for bit in partner_bits]
    extra_bits = [bit for bit in range(bit_count) if bit not in used]
    n, extra = 2 ** len(used), 2 ** len(extra_bits)
    planes, rows, gate = initial_state.shape
    owners = n // 2
    own = gate // owners
    held = n * (rows // owners)
    f32, bf16 = jnp.float32, jnp.bfloat16
    anywhere = pl.BlockSpec(memory_space=pl.ANY)
    return tuple(
        pl.pallas_call(
            functools.partial(kernel, used, order, extra_bits),
            out_shape=[jax.ShapeDtypeStruct(initial_state.shape, f32)] * 2,
            in_specs=[anywhere] * 3,
            out_specs=[anywhere] * 2,
            scratch_shapes=[
                pltpu.VMEM((2, held, gate), f32),
                pltpu.VMEM((2, held, gate), f32),
                pltpu.VMEM(current_gates.shape, f32),
                pltpu.VMEM((2, 2 * gate, held), bf16),
                pltpu.VMEM((2, held, gate), f32),
                pltpu.VMEM((2, held, gate), f32),
                pltpu.VMEM((SECTIONS, 2, gate, gate), f32),
                pltpu.VMEM((SECTIONS, owners, 2, own, gate), f32),
                pltpu.VMEM((SECTIONS, 2, gate, gate), f32),
                pltpu.VMEM((SECTIONS, extra, 2, own, gate), f32),
                pltpu.SemaphoreType.DMA((16, max(n, extra))),
                pltpu.SemaphoreType.DMA((16, max(n, extra))),
                pltpu.SemaphoreType.DMA((3,)),
            ],
            compiler_params=pltpu.CompilerParams(collective_id=0, has_side_effects=True),
            name="sweep",
        )(initial_state, adjoint_state, current_gates)
    )


def solution(mesh):
    return jax.shard_map(
        shards,
        mesh=mesh,
        in_specs=(
            P(None, ("groups", "long"), None),
            P(None, ("groups", "long"), None),
            P("groups", None, None, None),
        ),
        out_specs=(P(None, ("groups", "long"), None), P(None, ("groups", "long"), None)),
        check_vma=False,
    )
```

```python
import functools

import jax
import jax.numpy as jnp
from jax import lax
from jax.experimental import pallas as pl
from jax.experimental.pallas import tpu as pltpu
from jax.sharding import PartitionSpec as P

SECTIONS = 4
NS_ITERS = 8
MESH = pl.DeviceIdType.MESH
ADJ_IN, PSI_IN, RS, AG, MID, ADJ_OUT, PSI_OUT = 0, 1, 2, 6, 10, 14, 15


def split(x):
    high = x.astype(jnp.bfloat16)
    return high, (x - high.astype(jnp.float32)).astype(jnp.bfloat16)


def dot3(left, right, contract):
    def dot(a, b):
        return lax.dot_general(
            a, b, (contract, ((), ())), preferred_element_type=jnp.float32
        )

    return dot(left[0], right[0]) + (dot(left[0], right[1]) + dot(left[1], right[0]))


def embed_out(real, imag):
    return jnp.concatenate(
        [
            jnp.concatenate([real, -imag], axis=1),
            jnp.concatenate([imag, real], axis=1),
        ],
        axis=0,
    )


def swap_plane(plane, q, per):
    rows, lanes = plane.shape
    stride = per << q
    rolled = pltpu.roll(plane, lanes // 2, 1)
    low = lax.broadcasted_iota(jnp.int32, (stride, lanes), 1) < lanes // 2
    blocks = []
    for start in range(0, rows, 2 * stride):
        mid, end = start + stride, start + 2 * stride
        blocks.append(jnp.where(low, plane[start:mid], rolled[mid:end]))
        blocks.append(jnp.where(low, rolled[start:mid], plane[mid:end]))
    return jnp.concatenate(blocks, axis=0)


def swap(x, q, per):
    lanes = x.shape[1] // 2
    return jnp.concatenate(
        [swap_plane(x[:, :lanes], q, per), swap_plane(x[:, lanes:], q, per)], axis=1
    )


def polar(x, sweeps):
    gate = x.shape[0]
    norm = lax.rsqrt(jnp.sum(x * x, keepdims=True) + 1e-06)

    def sweep(_, a):
        high, low = split(a)

        def embed(v):
            real, imag = v[:, :gate], v[:, gate:]
            return jnp.concatenate([v, jnp.concatenate([-imag, real], axis=1)], axis=0)

        full = (embed(high), embed(low))
        def product(left, axis):
            def dot(u, v):
                return lax.dot_general(
                    u, v, (((1,), (axis,)), ((), ())), preferred_element_type=jnp.float32
                )

            both = dot(jnp.concatenate(left, axis=0), full[0])
            return both[:gate] + (both[gate:] + dot(left[0], full[1]))

        gram = product((high, low), 1)
        return 1.5 * a - 0.5 * product(split(gram), 0)

    return lax.fori_loop(0, sweeps, sweep, x * norm)


def kernel(
    used, order, extra_bits,
    psi_in, adj_in, gates_in, psi_out, adj_out,
    psi_buf, adj_buf, gates, phi_t, psi_send, adj_send,
    part, rs_buf, ag_buf, mid_buf,
    send_sem, recv_sem, local_sem,
):
    group = lax.axis_index("groups")
    me = lax.axis_index("long")
    n = 2 ** len(used)
    extra = 2 ** len(extra_bits)
    rows = psi_in.shape[1]
    gate = psi_in.shape[2]
    owners = n // 2
    first = n // 4
    own = gate // owners
    per = rows // owners

    def gather(value, bits):
        out = 0
        for k, bit in enumerate(bits):
            out = out + lax.rem(lax.div(value, 2**bit), 2) * 2**k
        return out

    def scatter(value, bits):
        out = 0
        for k, bit in enumerate(bits):
            out = out + lax.rem(lax.div(value, 2**k), 2) * 2**bit
        return out

    slot = gather(me, used)
    layer = gather(me, extra_bits)

    def peer(j):
        return scatter(j, used) + scatter(layer, extra_bits)

    def layer_peer(j):
        return scatter(slot, used) + scatter(j, extra_bits)

    def others(fn, mine=slot, count=n):
        def step(off, carry):
            fn(lax.rem(mine + off, count))
            return carry

        lax.fori_loop(1, count, step, 0)

    quarter = n // 4
    column = lax.div(slot, quarter)
    upper = lax.div(column, 2)
    inner = column + upper * (3 - 2 * column)

    def far_first(fn, ranks=(0, 1, 2, 3)):
        for rank in ranks:
            place = (3, 2, 1 - inner, inner)[rank]
            base = (place + upper * (3 - 2 * place)) * quarter

            def step(k, carry):
                fn(base + lax.rem(slot + 1 + k, quarter))
                return carry

            lax.fori_loop(0, quarter - (rank == 3), step, 0)

    def owners_far_first(fn, among=False):
        for rank in range(2):
            base = (2 - rank + upper * (2 * rank - 1)) * quarter

            def step(k, carry):
                fn(base + lax.rem(slot + 1 + k, quarter))
                return carry

            lax.fori_loop(0, quarter - rank, step, 0)

            if rank == 1 and not among:

                @pl.when(jnp.logical_not(is_owner))
                def _():
                    fn(base + lax.rem(slot, quarter))

    is_owner = inner == 1

    def remote(src, dst, phase, there, here, target):
        return pltpu.make_async_remote_copy(
            src_ref=src,
            dst_ref=dst,
            send_sem=send_sem.at[phase, there],
            recv_sem=recv_sem.at[phase, here],
            device_id={"groups": group, "long": target},
            device_id_type=MESH,
        )

    def block(ref, j, size):
        return ref.at[:, pl.ds(pl.multiple_of(j * size, size), size), :]

    index = slot - first

    def signal(j, target):
        pl.semaphore_signal(
            barrier, inc=1, device_id={"groups": group, "long": target(j)}, device_id_type=MESH
        )

    barrier = pltpu.get_barrier_semaphore()

    @pl.when(is_owner)
    def _():
        far_first(lambda j: signal(j, peer))
        if extra > 1:
            others(lambda j: signal(j, layer_peer), layer, extra)
        pl.semaphore_wait(barrier, n + extra - 2)

    @pl.when(jnp.logical_not(is_owner))
    def _():
        owners_far_first(lambda j: signal(j, peer))
        pl.semaphore_wait(barrier, owners)

    def inward(src, dst, phase):
        return lambda j: remote(
            block(src, j - first, per), block(dst, slot, per), phase, j, slot, peer(j)
        )

    def inward_from(dst, phase):
        return lambda j: remote(block(dst, j, per), block(dst, j, per), phase, j, j, peer(j))

    def outward(src, dst, phase):
        return lambda j: remote(
            block(src, j, per), block(dst, index, per), phase, j, slot, peer(j)
        )

    def outward_from(dst, phase):
        return lambda j: remote(
            block(dst, j - first, per), block(dst, j - first, per), phase, j, j, peer(j)
        )

    owners_far_first(lambda j: inward(adj_in, adj_buf, ADJ_IN)(j).start())
    owners_far_first(lambda j: inward(psi_in, psi_buf, PSI_IN)(j).start())

    def joined(ref):
        return jnp.concatenate([ref[0], ref[1]], axis=1)

    def put(ref, x):
        for q in order[::-1]:
            x = swap(x, q, per)
        ref[0] = x[:, :gate]
        ref[1] = x[:, gate:]

    def advance_adjoint(phi, s):
        full = split(embed_out(gates[s, 0], gates[s, 1]))
        phi = dot3(split(phi), full, ((1,), (1,)))
        high, low = split(phi.T)
        phi_t[s, 0] = high
        phi_t[s, 1] = low
        return phi

    @pl.when(is_owner)
    def _():
        gate_copy = pltpu.make_async_copy(gates_in, gates, local_sem.at[0])
        adj_own = pltpu.make_async_copy(block(adj_in, index, per), block(adj_buf, slot, per), local_sem.at[1])
        psi_own = pltpu.make_async_copy(block(psi_in, index, per), block(psi_buf, slot, per), local_sem.at[2])
        gate_copy.start()
        adj_own.start()
        psi_own.start()
        mine = pl.ds(pl.multiple_of(index * own, own), own)

        gate_copy.wait()
        adj_own.wait()
        others(lambda j: inward_from(adj_buf, ADJ_IN)(j).wait_recv())
        phi = joined(adj_buf)
        for s in range(SECTIONS):
            phi = advance_adjoint(swap(phi, order[s], per), s)
        put(adj_send, phi)
        adj_back = pltpu.make_async_copy(block(adj_send, slot, per), block(adj_out, index, per), local_sem.at[1])
        adj_back.start()
        psi_own.wait()
        others(lambda j: inward_from(psi_buf, PSI_IN)(j).wait_recv())
        psi = swap(joined(psi_buf), order[0], per)

        for s in range(SECTIONS):
            state = split(psi)
            outer = dot3((phi_t[s, 0], phi_t[s, 1]), state, ((1,), (0,)))
            part[s, 0] = outer[:gate, :gate] + outer[gate:, gate:]
            part[s, 1] = outer[gate:, :gate] - outer[:gate, gate:]

            def to_owner(j):
                return remote(
                    block(part.at[s], j - first, own), rs_buf.at[s, index], RS + s, j, slot, peer(j)
                )

            def from_owner(j):
                held = rs_buf.at[s, j - first]
                return remote(held, held, RS + s, j, j, peer(j))

            owners_far_first(lambda j: to_owner(j).start(), True)
            owners_far_first(lambda j: from_owner(j).wait_recv(), True)
            rs_buf[s, index] = part[s, :, mine, :]
            total = rs_buf[s, 0]
            for j in range(1, owners):
                total = total + rs_buf[s, j]
            if extra > 1:
                mid_buf[s, layer] = total

                def across(j, here):
                    held = mid_buf.at[s, here]
                    return remote(held, held, MID + s, j, here, layer_peer(j))

                others(lambda j: across(j, layer).start(), layer, extra)
                others(lambda j: across(j, j).wait_recv(), layer, extra)
                total = mid_buf[s, 0]
                for j in range(1, extra):
                    total = total + mid_buf[s, j]
            ag_buf[s, :, mine, :] = total
            held = block(ag_buf.at[s], index, own)
            owners_far_first(lambda j: remote(held, held, AG + s, j, slot, peer(j)).start(), True)

            def arrive(j):
                there = block(ag_buf.at[s], j - first, own)
                remote(there, there, AG + s, j, j, peer(j)).wait_recv()

            owners_far_first(arrive, True)
            if s < 3:
                back_ranks = ((2, 3), (0,), (1,))[s]
                far_first(lambda j: outward(adj_send, adj_out, ADJ_OUT)(j).start(), back_ranks)
            fitted = polar(jnp.concatenate([ag_buf[s, 0], ag_buf[s, 1]], axis=1), NS_ITERS)
            full = split(embed_out(fitted[:, :gate], fitted[:, gate:]))
            psi = dot3(state, full, ((1,), (1,)))
            if s + 1 < SECTIONS:
                psi = swap(psi, order[s + 1], per)

        put(psi_send, psi)
        far_first(lambda j: outward(psi_send, psi_out, PSI_OUT)(j).start())
        psi_back = pltpu.make_async_copy(block(psi_send, slot, per), block(psi_out, index, per), local_sem.at[2])
        psi_back.start()
        for s in range(SECTIONS):
            owners_far_first(
                lambda j: remote(block(part.at[s], j - first, own), rs_buf.at[s, index], RS + s, j, slot, peer(j)).wait_send(),
                True,
            )
            sent = block(ag_buf.at[s], index, own)
            owners_far_first(lambda j: remote(sent, sent, AG + s, j, slot, peer(j)).wait_send(), True)
            if extra > 1:
                done = mid_buf.at[s, layer]
                others(lambda j: remote(done, done, MID + s, j, layer, layer_peer(j)).wait_send(), layer, extra)
        adj_back.wait()
        psi_back.wait()
        others(lambda j: outward(adj_send, adj_out, ADJ_OUT)(j).wait_send())
        others(lambda j: outward(psi_send, psi_out, PSI_OUT)(j).wait_send())

    owners_far_first(lambda j: inward(adj_in, adj_buf, ADJ_IN)(j).wait_send())
    owners_far_first(lambda j: inward(psi_in, psi_buf, PSI_IN)(j).wait_send())
    owners_far_first(lambda j: outward_from(adj_out, ADJ_OUT)(j).wait_recv())
    owners_far_first(lambda j: outward_from(psi_out, PSI_OUT)(j).wait_recv())


def shards(initial_state, adjoint_state, current_gates):
    bit_count = lax.axis_size("long").bit_length() - 1
    partner_bits = [bit_count - 1, bit_count // 2, 0, 1]
    used = sorted(set(partner_bits))
    assert len(used) == SECTIONS
    order = [used.index(bit) for bit in partner_bits]
    extra_bits = [bit for bit in range(bit_count) if bit not in used]
    n, extra = 2 ** len(used), 2 ** len(extra_bits)
    planes, rows, gate = initial_state.shape
    owners = n // 2
    own = gate // owners
    held = n * (rows // owners)
    f32, bf16 = jnp.float32, jnp.bfloat16
    anywhere = pl.BlockSpec(memory_space=pl.ANY)
    return tuple(
        pl.pallas_call(
            functools.partial(kernel, used, order, extra_bits),
            out_shape=[jax.ShapeDtypeStruct(initial_state.shape, f32)] * 2,
            in_specs=[anywhere] * 3,
            out_specs=[anywhere] * 2,
            scratch_shapes=[
                pltpu.VMEM((2, held, gate), f32),
                pltpu.VMEM((2, held, gate), f32),
                pltpu.VMEM(current_gates.shape, f32),
                pltpu.VMEM((SECTIONS, 2, 2 * gate, held), bf16),
                pltpu.VMEM((2, held, gate), f32),
                pltpu.VMEM((2, held, gate), f32),
                pltpu.VMEM((SECTIONS, 2, gate, gate), f32),
                pltpu.VMEM((SECTIONS, owners, 2, own, gate), f32),
                pltpu.VMEM((SECTIONS, 2, gate, gate), f32),
                pltpu.VMEM((SECTIONS, extra, 2, own, gate), f32),
                pltpu.SemaphoreType.DMA((16, max(n, extra))),
                pltpu.SemaphoreType.DMA((16, max(n, extra))),
                pltpu.SemaphoreType.DMA((3,)),
            ],
            compiler_params=pltpu.CompilerParams(collective_id=0, has_side_effects=True),
            name="sweep",
        )(initial_state, adjoint_state, current_gates)
    )


def solution(mesh):
    return jax.shard_map(
        shards,
        mesh=mesh,
        in_specs=(
            P(None, ("groups", "long"), None),
            P(None, ("groups", "long"), None),
            P("groups", None, None, None),
        ),
        out_specs=(P(None, ("groups", "long"), None), P(None, ("groups", "long"), None)),
        check_vma=False,
    )
```

```python
import functools

import jax
import jax.numpy as jnp
from jax import lax
from jax.experimental import pallas as pl
from jax.experimental.pallas import tpu as pltpu
from jax.sharding import PartitionSpec as P

SECTIONS = 4
NS_ITERS = 8
MESH = pl.DeviceIdType.MESH
ADJ_IN, PSI_IN, RS, AG, MID, ADJ_OUT, PSI_OUT = 0, 1, 2, 6, 10, 14, 15


def split(x):
    high = x.astype(jnp.bfloat16)
    return high, (x - high.astype(jnp.float32)).astype(jnp.bfloat16)


def dot3(left, right, contract):
    def dot(a, b):
        return lax.dot_general(
            a, b, (contract, ((), ())), preferred_element_type=jnp.float32
        )

    return dot(left[0], right[0]) + (dot(left[0], right[1]) + dot(left[1], right[0]))


def embed_out(real, imag):
    return jnp.concatenate(
        [
            jnp.concatenate([real, -imag], axis=1),
            jnp.concatenate([imag, real], axis=1),
        ],
        axis=0,
    )


def swap_plane(plane, q, per):
    rows, lanes = plane.shape
    stride = per << q
    rolled = pltpu.roll(plane, lanes // 2, 1)
    low = lax.broadcasted_iota(jnp.int32, (stride, lanes), 1) < lanes // 2
    blocks = []
    for start in range(0, rows, 2 * stride):
        mid, end = start + stride, start + 2 * stride
        blocks.append(jnp.where(low, plane[start:mid], rolled[mid:end]))
        blocks.append(jnp.where(low, rolled[start:mid], plane[mid:end]))
    return jnp.concatenate(blocks, axis=0)


def swap(x, q, per):
    lanes = x.shape[1] // 2
    return jnp.concatenate(
        [swap_plane(x[:, :lanes], q, per), swap_plane(x[:, lanes:], q, per)], axis=1
    )


def polar(x, sweeps):
    gate = x.shape[0]
    norm = lax.rsqrt(jnp.sum(x * x, keepdims=True) + 1e-06)

    def sweep(_, a):
        high, low = split(a)

        def embed(v):
            real, imag = v[:, :gate], v[:, gate:]
            return jnp.concatenate([v, jnp.concatenate([-imag, real], axis=1)], axis=0)

        full = (embed(high), embed(low))
        def product(left, axis):
            def dot(u, v):
                return lax.dot_general(
                    u, v, (((1,), (axis,)), ((), ())), preferred_element_type=jnp.float32
                )

            both = dot(jnp.concatenate(left, axis=0), full[0])
            return both[:gate] + (both[gate:] + dot(left[0], full[1]))

        gram = product((high, low), 1)
        return 1.5 * a - 0.5 * product(split(gram), 0)

    return lax.fori_loop(0, sweeps, sweep, x * norm, unroll=8)


def kernel(
    used, order, extra_bits,
    psi_in, adj_in, gates_in, psi_out, adj_out,
    psi_buf, adj_buf, gates, phi_t, psi_send, adj_send,
    part, rs_buf, ag_buf, mid_buf,
    send_sem, recv_sem, local_sem,
):
    group = lax.axis_index("groups")
    me = lax.axis_index("long")
    n = 2 ** len(used)
    extra = 2 ** len(extra_bits)
    rows = psi_in.shape[1]
    gate = psi_in.shape[2]
    owners = n // 2
    first = n // 4
    own = gate // owners
    per = rows // owners

    def gather(value, bits):
        out = 0
        for k, bit in enumerate(bits):
            out = out + lax.rem(lax.div(value, 2**bit), 2) * 2**k
        return out

    def scatter(value, bits):
        out = 0
        for k, bit in enumerate(bits):
            out = out + lax.rem(lax.div(value, 2**k), 2) * 2**bit
        return out

    slot = gather(me, used)
    layer = gather(me, extra_bits)

    def peer(j):
        return scatter(j, used) + scatter(layer, extra_bits)

    def layer_peer(j):
        return scatter(slot, used) + scatter(j, extra_bits)

    def others(fn, mine=slot, count=n):
        def step(off, carry):
            fn(lax.rem(mine + off, count))
            return carry

        lax.fori_loop(1, count, step, 0)

    quarter = n // 4
    column = lax.div(slot, quarter)
    upper = lax.div(column, 2)
    inner = column + upper * (3 - 2 * column)

    def far_first(fn, ranks=(0, 1, 2, 3)):
        for rank in ranks:
            place = (3, 2, 1 - inner, inner)[rank]
            base = (place + upper * (3 - 2 * place)) * quarter

            def step(k, carry):
                fn(base + lax.rem(slot + 1 + k, quarter))
                return carry

            lax.fori_loop(0, quarter - (rank == 3), step, 0)

    def owners_far_first(fn, among=False):
        for rank in range(2):
            base = (2 - rank + upper * (2 * rank - 1)) * quarter

            def step(k, carry):
                fn(base + lax.rem(slot + 1 + k, quarter))
                return carry

            lax.fori_loop(0, quarter - rank, step, 0)

            if rank == 1 and not among:

                @pl.when(jnp.logical_not(is_owner))
                def _():
                    fn(base + lax.rem(slot, quarter))

    is_owner = inner == 1

    def remote(src, dst, phase, there, here, target):
        return pltpu.make_async_remote_copy(
            src_ref=src,
            dst_ref=dst,
            send_sem=send_sem.at[phase, there],
            recv_sem=recv_sem.at[phase, here],
            device_id={"groups": group, "long": target},
            device_id_type=MESH,
        )

    def block(ref, j, size):
        return ref.at[:, pl.ds(pl.multiple_of(j * size, size), size), :]

    index = slot - first

    def signal(j, target):
        pl.semaphore_signal(
            barrier, inc=1, device_id={"groups": group, "long": target(j)}, device_id_type=MESH
        )

    barrier = pltpu.get_barrier_semaphore()

    @pl.when(is_owner)
    def _():
        far_first(lambda j: signal(j, peer))
        if extra > 1:
            others(lambda j: signal(j, layer_peer), layer, extra)
        pl.semaphore_wait(barrier, n + extra - 2)

    @pl.when(jnp.logical_not(is_owner))
    def _():
        owners_far_first(lambda j: signal(j, peer))
        pl.semaphore_wait(barrier, owners)

    def inward(src, dst, phase):
        return lambda j: remote(
            block(src, j - first, per), block(dst, slot, per), phase, j, slot, peer(j)
        )

    def inward_from(dst, phase):
        return lambda j: remote(block(dst, j, per), block(dst, j, per), phase, j, j, peer(j))

    def outward(src, dst, phase):
        return lambda j: remote(
            block(src, j, per), block(dst, index, per), phase, j, slot, peer(j)
        )

    def outward_from(dst, phase):
        return lambda j: remote(
            block(dst, j - first, per), block(dst, j - first, per), phase, j, j, peer(j)
        )

    owners_far_first(lambda j: inward(adj_in, adj_buf, ADJ_IN)(j).start())
    owners_far_first(lambda j: inward(psi_in, psi_buf, PSI_IN)(j).start())

    def joined(ref):
        return jnp.concatenate([ref[0], ref[1]], axis=1)

    def put(ref, x):
        for q in order[::-1]:
            x = swap(x, q, per)
        ref[0] = x[:, :gate]
        ref[1] = x[:, gate:]

    def advance_adjoint(phi, s):
        full = split(embed_out(gates[s, 0], gates[s, 1]))
        phi = dot3(split(phi), full, ((1,), (1,)))
        high, low = split(phi.T)
        phi_t[s, 0] = high
        phi_t[s, 1] = low
        return phi

    @pl.when(is_owner)
    def _():
        gate_copy = pltpu.make_async_copy(gates_in, gates, local_sem.at[0])
        adj_own = pltpu.make_async_copy(block(adj_in, index, per), block(adj_buf, slot, per), local_sem.at[1])
        psi_own = pltpu.make_async_copy(block(psi_in, index, per), block(psi_buf, slot, per), local_sem.at[2])
        gate_copy.start()
        adj_own.start()
        psi_own.start()
        mine = pl.ds(pl.multiple_of(index * own, own), own)

        gate_copy.wait()
        adj_own.wait()
        others(lambda j: inward_from(adj_buf, ADJ_IN)(j).wait_recv())
        phi = joined(adj_buf)
        for s in range(SECTIONS):
            phi = advance_adjoint(swap(phi, order[s], per), s)
        put(adj_send, phi)
        adj_back = pltpu.make_async_copy(block(adj_send, slot, per), block(adj_out, index, per), local_sem.at[1])
        adj_back.start()
        psi_own.wait()
        others(lambda j: inward_from(psi_buf, PSI_IN)(j).wait_recv())
        psi = swap(joined(psi_buf), order[0], per)

        for s in range(SECTIONS):
            state = split(psi)
            outer = dot3((phi_t[s, 0], phi_t[s, 1]), state, ((1,), (0,)))
            part[s, 0] = outer[:gate, :gate] + outer[gate:, gate:]
            part[s, 1] = outer[gate:, :gate] - outer[:gate, gate:]

            def to_owner(j):
                return remote(
                    block(part.at[s], j - first, own), rs_buf.at[s, index], RS + s, j, slot, peer(j)
                )

            def from_owner(j):
                held = rs_buf.at[s, j - first]
                return remote(held, held, RS + s, j, j, peer(j))

            owners_far_first(lambda j: to_owner(j).start(), True)
            owners_far_first(lambda j: from_owner(j).wait_recv(), True)
            rs_buf[s, index] = part[s, :, mine, :]
            total = rs_buf[s, 0]
            for j in range(1, owners):
                total = total + rs_buf[s, j]
            if extra > 1:
                mid_buf[s, layer] = total

                def across(j, here):
                    held = mid_buf.at[s, here]
                    return remote(held, held, MID + s, j, here, layer_peer(j))

                others(lambda j: across(j, layer).start(), layer, extra)
                others(lambda j: across(j, j).wait_recv(), layer, extra)
                total = mid_buf[s, 0]
                for j in range(1, extra):
                    total = total + mid_buf[s, j]
            ag_buf[s, :, mine, :] = total
            held = block(ag_buf.at[s], index, own)
            owners_far_first(lambda j: remote(held, held, AG + s, j, slot, peer(j)).start(), True)

            def arrive(j):
                there = block(ag_buf.at[s], j - first, own)
                remote(there, there, AG + s, j, j, peer(j)).wait_recv()

            owners_far_first(arrive, True)
            if s < 3:
                back_ranks = ((2, 3), (0,), (1,))[s]
                far_first(lambda j: outward(adj_send, adj_out, ADJ_OUT)(j).start(), back_ranks)
            fitted = polar(jnp.concatenate([ag_buf[s, 0], ag_buf[s, 1]], axis=1), NS_ITERS)
            full = split(embed_out(fitted[:, :gate], fitted[:, gate:]))
            psi = dot3(state, full, ((1,), (1,)))
            if s + 1 < SECTIONS:
                psi = swap(psi, order[s + 1], per)

        put(psi_send, psi)
        far_first(lambda j: outward(psi_send, psi_out, PSI_OUT)(j).start())
        psi_back = pltpu.make_async_copy(block(psi_send, slot, per), block(psi_out, index, per), local_sem.at[2])
        psi_back.start()
        for s in range(SECTIONS):
            owners_far_first(
                lambda j: remote(block(part.at[s], j - first, own), rs_buf.at[s, index], RS + s, j, slot, peer(j)).wait_send(),
                True,
            )
            sent = block(ag_buf.at[s], index, own)
            owners_far_first(lambda j: remote(sent, sent, AG + s, j, slot, peer(j)).wait_send(), True)
            if extra > 1:
                done = mid_buf.at[s, layer]
                others(lambda j: remote(done, done, MID + s, j, layer, layer_peer(j)).wait_send(), layer, extra)
        adj_back.wait()
        psi_back.wait()
        others(lambda j: outward(adj_send, adj_out, ADJ_OUT)(j).wait_send())
        others(lambda j: outward(psi_send, psi_out, PSI_OUT)(j).wait_send())

    owners_far_first(lambda j: inward(adj_in, adj_buf, ADJ_IN)(j).wait_send())
    owners_far_first(lambda j: inward(psi_in, psi_buf, PSI_IN)(j).wait_send())
    owners_far_first(lambda j: outward_from(adj_out, ADJ_OUT)(j).wait_recv())
    owners_far_first(lambda j: outward_from(psi_out, PSI_OUT)(j).wait_recv())


def shards(initial_state, adjoint_state, current_gates):
    bit_count = lax.axis_size("long").bit_length() - 1
    partner_bits = [bit_count - 1, bit_count // 2, 0, 1]
    used = sorted(set(partner_bits))
    assert len(used) == SECTIONS
    order = [used.index(bit) for bit in partner_bits]
    extra_bits = [bit for bit in range(bit_count) if bit not in used]
    n, extra = 2 ** len(used), 2 ** len(extra_bits)
    planes, rows, gate = initial_state.shape
    owners = n // 2
    own = gate // owners
    held = n * (rows // owners)
    f32, bf16 = jnp.float32, jnp.bfloat16
    anywhere = pl.BlockSpec(memory_space=pl.ANY)
    return tuple(
        pl.pallas_call(
            functools.partial(kernel, used, order, extra_bits),
            out_shape=[pltpu.VMEM(initial_state.shape, f32)] * 2,
            in_specs=[anywhere] * 3,
            out_specs=[pl.BlockSpec(memory_space=pltpu.VMEM)] * 2,
            scratch_shapes=[
                pltpu.VMEM((2, held, gate), f32),
                pltpu.VMEM((2, held, gate), f32),
                pltpu.VMEM(current_gates.shape, f32),
                pltpu.VMEM((SECTIONS, 2, 2 * gate, held), bf16),
                pltpu.VMEM((2, held, gate), f32),
                pltpu.VMEM((2, held, gate), f32),
                pltpu.VMEM((SECTIONS, 2, gate, gate), f32),
                pltpu.VMEM((SECTIONS, owners, 2, own, gate), f32),
                pltpu.VMEM((SECTIONS, 2, gate, gate), f32),
                pltpu.VMEM((SECTIONS, extra, 2, own, gate), f32),
                pltpu.SemaphoreType.DMA((16, max(n, extra))),
                pltpu.SemaphoreType.DMA((16, max(n, extra))),
                pltpu.SemaphoreType.DMA((3,)),
            ],
            compiler_params=pltpu.CompilerParams(collective_id=0, has_side_effects=True),
            name="sweep",
        )(initial_state, adjoint_state, current_gates)
    )


def solution(mesh):
    return jax.shard_map(
        shards,
        mesh=mesh,
        in_specs=(
            P(None, ("groups", "long"), None),
            P(None, ("groups", "long"), None),
            P("groups", None, None, None),
        ),
        out_specs=(P(None, ("groups", "long"), None), P(None, ("groups", "long"), None)),
        check_vma=False,
    )
```
